32 devices in a mesh: fsdp: 32 (over z, y, x, core).
Axes of the slice: x: 2, y: 2, z: 4, core: 2. Of those that a mesh axis runs over, the one named last changes fastest.
Arguments:
- images: bfloat16 [32, 196, 512], P('fsdp'), may hold values from -90 to 90
- cotangent: bfloat16 [32, 196, 512], P('fsdp'), may hold values from -6 to 6
- counts: int32 [32], P('fsdp'), may hold values from 0 to 1, as said below
- attn_gain: bfloat16 [2, 512], P(None, 'fsdp'), may hold values from 0.099609375 to 1.8984375
- attn_bias: bfloat16 [2, 512], P(None, 'fsdp'), may hold values from -3 to 3
- qkv_weight: bfloat16 [2, 512, 1536], P(None, 'fsdp'), may hold values from -0.25 to 0.25
- qv_bias: bfloat16 [2, 2, 512], P(None, None, 'fsdp'), may hold values from -3 to 3
- rel_table: bfloat16 [2, 192, 16], P(None, 'fsdp'), may hold values from -320 to 320
- proj_weight: bfloat16 [2, 512, 512], P(None, 'fsdp'), may hold values from -2 to 2
- proj_bias: bfloat16 [2, 512], P(None, 'fsdp'), may hold values from -3 to 3
- mlp_gain: bfloat16 [2, 512], P(None, 'fsdp'), may hold values from 0.099609375 to 1.8984375
- mlp_bias: bfloat16 [2, 512], P(None, 'fsdp'), may hold values from -3 to 3
- fc1_weight: bfloat16 [2, 512, 2048], P(None, 'fsdp'), may hold values from -0.25 to 0.25
- fc1_bias: bfloat16 [2, 2048], P(None, 'fsdp'), may hold values from -3 to 3
- fc2_weight: bfloat16 [2, 2048, 512], P(None, 'fsdp'), may hold values from -0.125 to 0.125
- fc2_bias: bfloat16 [2, 512], P(None, 'fsdp'), may hold values from -3 to 3
Outputs:
- out_tokens: float32 [32, 196, 512], P('fsdp')
- in_grad: float32 [32, 196, 512], P('fsdp')
- grad_attn_gain: float32 [2, 512], P(None, 'fsdp')
- grad_attn_bias: float32 [2, 512], P(None, 'fsdp')
- grad_qkv_weight: float32 [2, 512, 1536], P(None, 'fsdp')
- grad_qv_bias: float32 [2, 2, 512], P(None, None, 'fsdp')
- grad_rel_table: float32 [2, 192, 16], P(None, 'fsdp')
- grad_proj_weight: float32 [2, 512, 512], P(None, 'fsdp')
- grad_proj_bias: float32 [2, 512], P(None, 'fsdp')
- grad_mlp_gain: float32 [2, 512], P(None, 'fsdp')
- grad_mlp_bias: float32 [2, 512], P(None, 'fsdp')
- grad_fc1_weight: float32 [2, 512, 2048], P(None, 'fsdp')
- grad_fc1_bias: float32 [2, 2048], P(None, 'fsdp')
- grad_fc2_weight: float32 [2, 2048, 512], P(None, 'fsdp')
- grad_fc2_bias: float32 [2, 512], P(None, 'fsdp')
The draws below stay inside these ranges and needn't reach their ends.
Inputs may be any that keep to these rules, and one draw needn't show every extreme that they name: `counts`: every draw has a device with 1 images and a device with 0.
All inputs are finite; a program needn't handle non-finite values.
Results may differ from the reference program's by a relative error of at most 0.014.
The reference program's roundings to bfloat16 on the way count: a program that leaves them out, or rounds other values in their place, can miss the bound.
Values may be sent and summed in bfloat16 or wider, within the bound.
A program may use at most 128 MiB of HBM per device.

```python
import jax
import jax.numpy as jnp
from jax import lax

D = 512
HEADS = 16
MLP_UNITS = 2048
WIN = 7
SIDE = 14
LAYERS = 2
IMG_DEV = 1
SHIFT = 3
TOK_IMG = 196
SLOTS = 32
HOLDERS = 32
TABLE_ROWS = 192


def draw_images(key, part):
    key_base = jax.random.fold_in(key, 21)
    key_rows = jax.random.fold_in(key, 22)
    key_cols = jax.random.fold_in(key, 23)
    shape_all = (SLOTS, SIDE * SIDE, D)
    row_scale = jnp.exp(jax.random.uniform(key_rows, (SLOTS, SIDE * SIDE, 1), jnp.float32, -1.2, 1.2))
    col_scale = jnp.exp(jax.random.uniform(key_cols, (1, 1, D), jnp.float32, -1.2, 1.2))
    base = jnp.clip(jax.random.normal(key_base, shape_all, jnp.float32), -6.5, 6.5)
    return (base * row_scale * col_scale).astype(jnp.bfloat16)


def draw_counts(key, part):
    key_base = jax.random.fold_in(key, 31)
    key_full = jax.random.fold_in(key, 32)
    key_short = jax.random.fold_in(key, 33)
    drawn = jax.random.randint(key_base, (HOLDERS,), IMG_DEV - 1, IMG_DEV + 1)
    full_at = jax.random.randint(key_full, (), 0, HOLDERS)
    short_at = (full_at + 1 + jax.random.randint(key_short, (), 0, HOLDERS - 1)) % HOLDERS
    places = jnp.arange(HOLDERS, dtype=jnp.int32)
    drawn = jnp.where(places == full_at, IMG_DEV, drawn)
    drawn = jnp.where(places == short_at, IMG_DEV - 1, drawn)
    return drawn.astype(jnp.int32)


def draw_rel_table(key, part):
    key_base = jax.random.fold_in(key, 41)
    shape_all = (LAYERS, TABLE_ROWS, HEADS)
    values = jnp.clip(jax.random.normal(key_base, shape_all, jnp.float32), -6.0, 6.0)
    return values.astype(jnp.bfloat16)


def block_scale(key, extent, split, low, top_value):
    loudness = 1.0
    for axis_at, blocks in split:
        steps = jax.random.uniform(jax.random.fold_in(jax.random.fold_in(key, 6), axis_at), (blocks,), jnp.float32, low / len(split), top_value / len(split))
        loudness = loudness * jnp.repeat(jnp.exp(steps), extent[axis_at] // blocks).reshape((-1,) + (1,) * (len(extent) - 1 - axis_at))
    return loudness


def bell_draw(key, dims, deviation, most, split=(), kind=jnp.bfloat16):
    array = jax.random.normal(key, dims, jnp.float32) * deviation
    if len(split) > 0:
        array = block_scale(key, dims, split, -0.22, 0.18) * array
    return jnp.clip(array, min=-most, max=most).astype(kind)


def setup_inputs(seed: int = 0) -> dict:
    streams_of = jax.random.split(jax.random.key(seed), 17)
    return {
        "images": draw_images(jax.random.fold_in(streams_of[16], 71), 0),
        "cotangent": bell_draw(streams_of[1], (SLOTS, TOK_IMG, D), 1.0, 6.0, ((0, 32),)),
        "counts": draw_counts(jax.random.fold_in(streams_of[16], 71), 0),
        "attn_gain": jnp.clip(1.0 + 0.18 * jax.random.normal(streams_of[3], (LAYERS, D), jnp.float32), 0.099609375, 1.8984375).astype(jnp.bfloat16),
        "attn_bias": bell_draw(streams_of[4], (LAYERS, D), 0.5, 3.0, ((1, 32),)),
        "qkv_weight": bell_draw(streams_of[5], (LAYERS, D, 3 * D), D ** -0.5, 0.25, ((1, 32),)),
        "qv_bias": bell_draw(streams_of[6], (LAYERS, 2, D), 0.5, 3.0, ((2, 32),)),
        "rel_table": draw_rel_table(jax.random.fold_in(streams_of[16], 71), 0),
        "proj_weight": bell_draw(streams_of[8], (LAYERS, D, D), (D // (WIN * WIN)) ** -0.5, 2.0, ((1, 32),)),
        "proj_bias": bell_draw(streams_of[9], (LAYERS, D), 0.5, 3.0, ((1, 32),)),
        "mlp_gain": jnp.clip(1.0 + 0.18 * jax.random.normal(streams_of[10], (LAYERS, D), jnp.float32), 0.099609375, 1.8984375).astype(jnp.bfloat16),
        "mlp_bias": bell_draw(streams_of[11], (LAYERS, D), 0.5, 3.0, ((1, 32),)),
        "fc1_weight": bell_draw(streams_of[12], (LAYERS, D, MLP_UNITS), D ** -0.5, 0.25, ((1, 32),)),
        "fc1_bias": bell_draw(streams_of[13], (LAYERS, MLP_UNITS), 0.5, 3.0, ((1, 32),)),
        "fc2_weight": bell_draw(streams_of[14], (LAYERS, MLP_UNITS, D), MLP_UNITS ** -0.5, 0.125, ((1, 32),)),
        "fc2_bias": bell_draw(streams_of[15], (LAYERS, D), 0.5, 3.0, ((1, 32),)),
    }


norm_eps = 1e-05
mask_fill = -10000.0
highest = lax.Precision.HIGHEST
half_root = 0.7071067811865476
inv_root_tau = 0.3989422804014327

def layer_norm(rows, gain, offset):
    centre = lax.optimization_barrier(jnp.mean(rows, axis=-1, keepdims=True))
    centred = rows - centre
    spread = lax.optimization_barrier(jnp.mean(centred * centred, axis=-1, keepdims=True))
    return centred * lax.rsqrt(spread + norm_eps) * gain + offset

def gelu_slope(values):
    cumul = 0.5 * (1.0 + lax.erf(values * half_root))
    density = jnp.exp(-0.5 * values * values) * inv_root_tau
    return cumul + values * density

def batched(form, left, right):
    return jnp.einsum(form, left.astype(jnp.float32), right.astype(jnp.float32))

def to_windows(rows, shift_by):
    channels = rows.shape[-1]
    grid = rows.reshape(SIDE, SIDE, channels)
    if shift_by:
        grid = jnp.roll(grid, (-shift_by, -shift_by), axis=(0, 1))
    across = SIDE // WIN
    grid = grid.reshape(across, WIN, across, WIN, channels).transpose(0, 2, 1, 3, 4)
    return grid.reshape(across * across, WIN * WIN, channels)

def from_windows(blocks, shift_by):
    channels = blocks.shape[-1]
    across = SIDE // WIN
    grid = blocks.reshape(across, across, WIN, WIN, channels).transpose(0, 2, 1, 3, 4)
    grid = grid.reshape(SIDE, SIDE, channels)
    if shift_by:
        grid = jnp.roll(grid, (shift_by, shift_by), axis=(0, 1))
    return grid.reshape(SIDE * SIDE, channels)

def offset_onehot(table_rows):
    places = jnp.arange(WIN * WIN, dtype=jnp.int32)
    row_at = places // WIN
    col_at = places % WIN
    index = (row_at[:, None] - row_at[None, :] + WIN - 1) * (2 * WIN - 1) + (col_at[:, None] - col_at[None, :] + WIN - 1)
    targets = jnp.arange(table_rows, dtype=jnp.int32)
    return (index.reshape(-1)[:, None] == targets[None, :]).astype(jnp.float32)

def block_mask(shift_by):
    across = SIDE // WIN
    if not shift_by:
        return jnp.zeros((across * across, WIN * WIN, WIN * WIN), jnp.float32)
    coord = jnp.arange(SIDE, dtype=jnp.int32)
    region = jnp.where(coord < SIDE - WIN, 0, jnp.where(coord < SIDE - shift_by, 1, 2)).astype(jnp.int32)
    labels = (region[:, None] * 3 + region[None, :]).reshape(SIDE * SIDE, 1)
    labels = to_windows(labels, 0)[:, :, 0]
    return jnp.where(labels[:, :, None] == labels[:, None, :], 0.0, mask_fill).astype(jnp.float32)

def attend_scores(query, keys, pos_bias, mask_add, scaling):
    scores = batched('nqhd,nkhd->nhqk', query, keys) * scaling
    return scores + pos_bias[None] + mask_add[:, None]

def block_forward(current, layer_weights, onehot, mask_add, shift_by):
    gain_one, bias_one, w_qkv, b_qv, table, w_proj, b_proj, gain_two, bias_two, w_first, b_first, w_second, b_second = layer_weights
    features = current.shape[-1]
    head_count = table.shape[-1]
    head_size = features // head_count
    scaling = head_size ** (-0.5)
    normed = layer_norm(current, gain_one.astype(jnp.float32), bias_one.astype(jnp.float32)).astype(jnp.bfloat16)
    windowed = to_windows(normed, shift_by)
    win_count, win_len = (windowed.shape[0], windowed.shape[1])
    flat_in = windowed.reshape(win_count * win_len, features)
    full_bias = jnp.concatenate([b_qv[0].astype(jnp.float32), jnp.zeros((features,), jnp.float32), b_qv[1].astype(jnp.float32)])
    packed = (jnp.dot(flat_in, w_qkv, preferred_element_type=jnp.float32) + full_bias).astype(jnp.bfloat16)
    packed = packed.reshape(win_count, win_len, 3, head_count, head_size)
    query, keys, values = (packed[:, :, 0], packed[:, :, 1], packed[:, :, 2])
    pos_bias = jnp.dot(onehot, table.astype(jnp.float32), precision=highest)
    pos_bias = pos_bias.reshape(win_len, win_len, head_count).transpose(2, 0, 1)
    scores = attend_scores(query, keys, pos_bias, mask_add, scaling)
    peak = lax.optimization_barrier(jnp.max(scores, axis=-1, keepdims=True))
    log_total = peak + jnp.log(lax.optimization_barrier(jnp.sum(jnp.exp(scores - peak), axis=-1, keepdims=True)))
    probs = jnp.exp(scores - log_total).astype(jnp.bfloat16)
    mixed = batched('nhqk,nkhd->nqhd', probs, values).astype(jnp.bfloat16).reshape(win_count * win_len, features)
    attended = jnp.dot(mixed, w_proj, preferred_element_type=jnp.float32) + b_proj.astype(jnp.float32)
    middle = current + from_windows(attended.reshape(win_count, win_len, features), shift_by)
    second_in = layer_norm(middle, gain_two.astype(jnp.float32), bias_two.astype(jnp.float32)).astype(jnp.bfloat16)
    pre_act = jnp.dot(second_in, w_first, preferred_element_type=jnp.float32) + b_first.astype(jnp.float32)
    activ = jax.nn.gelu(pre_act, approximate=False).astype(jnp.bfloat16)
    after = middle + jnp.dot(activ, w_second, preferred_element_type=jnp.float32) + b_second.astype(jnp.float32)
    memo = (current, flat_in, query, keys, values, pos_bias, log_total, mixed, middle, second_in, pre_act, activ)
    return (after, memo)

def block_backward(grad_rows, layer_weights, memo, onehot, mask_add, shift_by):
    gain_one, bias_one, w_qkv, b_qv, table, w_proj, b_proj, gain_two, bias_two, w_first, b_first, w_second, b_second = layer_weights
    current, flat_in, query, keys, values, pos_bias, log_total, mixed, middle, second_in, pre_act, activ = memo
    features = current.shape[-1]
    head_count = table.shape[-1]
    head_size = features // head_count
    scaling = head_size ** (-0.5)
    win_count, win_len = (query.shape[0], query.shape[1])
    grad_low = grad_rows.astype(jnp.bfloat16)
    g_second = jnp.dot(activ.T, grad_low, preferred_element_type=jnp.float32)
    g_b_second = lax.optimization_barrier(jnp.sum(grad_rows, axis=0))
    grad_pre = jnp.dot(grad_low, w_second.T, preferred_element_type=jnp.float32) * gelu_slope(pre_act)
    g_b_first = lax.optimization_barrier(jnp.sum(grad_pre, axis=0))
    pre_low = grad_pre.astype(jnp.bfloat16)
    g_first = jnp.dot(second_in.T, pre_low, preferred_element_type=jnp.float32)
    grad_norm_two = jnp.dot(pre_low, w_first.T, preferred_element_type=jnp.float32)
    unused, pull_two = jax.vjp(layer_norm, middle, gain_two.astype(jnp.float32), bias_two.astype(jnp.float32))
    back_mid, g_gain_two, g_bias_two = pull_two(grad_norm_two)
    grad_middle = grad_rows + back_mid
    attn_low = to_windows(grad_middle, shift_by).reshape(win_count * win_len, features).astype(jnp.bfloat16)
    g_proj = jnp.dot(mixed.T, attn_low, preferred_element_type=jnp.float32)
    g_b_proj = lax.optimization_barrier(jnp.sum(grad_middle, axis=0))
    grad_mixed = jnp.dot(attn_low, w_proj.T, preferred_element_type=jnp.float32).astype(jnp.bfloat16)
    grad_mixed = grad_mixed.reshape(win_count, win_len, head_count, head_size)
    scores = attend_scores(query, keys, pos_bias, mask_add, scaling)
    probs_full = jnp.exp(scores - log_total)
    grad_probs = batched('nqhd,nkhd->nhqk', grad_mixed, values)
    grad_values = batched('nhqk,nqhd->nkhd', probs_full.astype(jnp.bfloat16), grad_mixed)
    grad_scores = probs_full * (grad_probs - lax.optimization_barrier(jnp.sum(probs_full * grad_probs, axis=-1, keepdims=True)))
    per_pair = lax.optimization_barrier(jnp.sum(grad_scores, axis=0)).reshape(head_count, win_len * win_len)
    g_table = jnp.dot(per_pair, onehot, precision=highest).T
    scores_low = grad_scores.astype(jnp.bfloat16)
    grad_query = batched('nhqk,nkhd->nqhd', scores_low, keys) * scaling
    grad_keys = batched('nhqk,nqhd->nkhd', scores_low, query) * scaling
    g_qv = jnp.stack([lax.optimization_barrier(jnp.sum(grad_query, axis=(0, 1))).reshape(features), lax.optimization_barrier(jnp.sum(grad_values, axis=(0, 1))).reshape(features)])
    grad_packed = jnp.stack([grad_query, grad_keys, grad_values], axis=2).reshape(win_count * win_len, 3 * features).astype(jnp.bfloat16)
    g_qkv = jnp.dot(flat_in.T, grad_packed, preferred_element_type=jnp.float32)
    grad_norm_one = jnp.dot(grad_packed, w_qkv.T, preferred_element_type=jnp.float32)
    grad_norm_one = from_windows(grad_norm_one.reshape(win_count, win_len, features), shift_by)
    unused_too, pull_one = jax.vjp(layer_norm, current, gain_one.astype(jnp.float32), bias_one.astype(jnp.float32))
    back_in, g_gain_one, g_bias_one = pull_one(grad_norm_one)
    grad_terms = (g_gain_one, g_bias_one, g_qkv, g_qv, g_table, g_proj, g_b_proj, g_gain_two, g_bias_two, g_first, g_b_first, g_second, g_b_second)
    return (grad_middle + back_in, grad_terms)

def image_forward(picture, weights, onehot):
    current = picture.astype(jnp.float32)
    history = []
    for layer_idx in range(LAYERS):
        shift_by = SHIFT if layer_idx % 2 else 0
        layer_weights = tuple((tensor[layer_idx] for tensor in weights))
        current, memo = block_forward(current, layer_weights, onehot, block_mask(shift_by), shift_by)
        history.append(memo)
    return (current, history)

def image_backward(grad_rows, weights, history, onehot):
    layer_grads = [None] * LAYERS
    for layer_idx in reversed(range(LAYERS)):
        shift_by = SHIFT if layer_idx % 2 else 0
        layer_weights = tuple((tensor[layer_idx] for tensor in weights))
        grad_rows, layer_grads[layer_idx] = block_backward(grad_rows, layer_weights, history[layer_idx], onehot, block_mask(shift_by), shift_by)
    stacked = jax.tree.map(lambda *pieces: jnp.stack(pieces), *layer_grads)
    return (grad_rows, stacked)

def reference(images, cotangent, counts, attn_gain, attn_bias, qkv_weight, qv_bias, rel_table, proj_weight, proj_bias, mlp_gain, mlp_bias, fc1_weight, fc1_bias, fc2_weight, fc2_bias):
    weights = (attn_gain, attn_bias, qkv_weight, qv_bias, rel_table, proj_weight, proj_bias, mlp_gain, mlp_bias, fc1_weight, fc1_bias, fc2_weight, fc2_bias)
    onehot = offset_onehot(TABLE_ROWS)
    slot_ids = jnp.arange(SLOTS, dtype=jnp.int32)
    active_all = slot_ids % IMG_DEV < counts[slot_ids // IMG_DEV]
    totals = tuple((jnp.zeros(tensor.shape, jnp.float32) for tensor in weights))

    def advance(running, record):
        picture, upstream, active = record
        output_rows, history = image_forward(picture, weights, onehot)
        shown = jnp.where(active, output_rows, 0.0)
        seed_grad = jnp.where(active, upstream.astype(jnp.float32), 0.0)
        grad_in, grad_terms = image_backward(seed_grad, weights, history, onehot)
        running = tuple((left + right for left, right in zip(running, grad_terms)))
        return (running, (shown, grad_in))
    running, (outs, grads_in) = lax.scan(advance, totals, (images, cotangent, active_all))
    return (outs, grads_in, running[0], running[1], running[2], running[3], running[4], running[5], running[6], running[7], running[8], running[9], running[10], running[11], running[12])
```

```python
import functools

import jax
import jax.numpy as jnp
from jax import lax
from jax.experimental import pallas as pl
from jax.experimental.pallas import tpu as pltpu
from jax.sharding import PartitionSpec as P

WIN = 7
SIDE = 14
LAYERS = 2
SHIFT = 3

norm_eps = 1e-05
mask_fill = -10000.0
outside_fill = -1e30
half_root = 0.7071067811865476
inv_root_tau = 0.3989422804014327
lanes = 128
bf16 = jnp.bfloat16
f32 = jnp.float32


def dot_nn(left, right):
    return lax.dot_general(left, right, (((1,), (0,)), ((), ())), preferred_element_type=f32)


def dot_nt(left, right):
    return lax.dot_general(left, right, (((1,), (1,)), ((), ())), preferred_element_type=f32)


def dot_tn(left, right):
    return lax.dot_general(left, right, (((0,), (0,)), ((), ())), preferred_element_type=f32)


def normalize(rows):
    centred = rows - jnp.mean(rows, axis=-1, keepdims=True)
    spread = jnp.mean(centred * centred, axis=-1, keepdims=True)
    inverse = lax.rsqrt(spread + norm_eps)
    return centred * inverse, inverse


def norm_pull(rows, gain, grad):
    unit, inverse = normalize(rows)
    g_gain = jnp.sum(grad * unit, axis=0, keepdims=True)
    g_bias = jnp.sum(grad, axis=0, keepdims=True)
    scaled = grad * gain
    back = inverse * (
        scaled
        - jnp.mean(scaled, axis=-1, keepdims=True)
        - unit * jnp.mean(scaled * unit, axis=-1, keepdims=True)
    )
    return back, g_gain, g_bias


def head_mask(local_head, head_size):
    lane = lax.broadcasted_iota(jnp.int32, (1, lanes), 1)
    return jnp.where(lane // head_size == local_head, 1.0, 0.0).astype(bf16)


def bias_kernel(pairs_ref, spread_ref, spread_t_ref, mask_ref, out_ref):
    def step(head, carry):
        rows = dot_nn(spread_ref[...], pairs_ref[head]).astype(bf16)
        out_ref[head] = dot_nn(rows, spread_t_ref[...]) + mask_ref[...]
        return carry

    lax.fori_loop(0, pairs_ref.shape[0], step, 0)


def attn_fwd_kernel(
    x_ref, gain_ref, off_ref, wqkv_ref, bqkv_ref, bias_ref, wproj_ref, bproj_ref,
    mid_ref, xn_ref, qkv_ref, key_t_ref, probs_ref, mixed_t_ref,
    val_t,
):
    rows = x_ref[...]
    features = rows.shape[1]
    heads = bias_ref.shape[0]
    size = features // heads
    scaling = size ** (-0.5)
    unit, _ = normalize(rows)
    xn = (unit * gain_ref[...] + off_ref[...]).astype(bf16)
    xn_ref[...] = xn
    for part in range(3):
        cols = pl.ds(part * features, features)
        block = dot_nn(xn, wqkv_ref[:, cols]) + bqkv_ref[:, cols]
        qkv_ref[:, cols] = block.astype(bf16)
        if part == 1:
            key_t_ref[...] = block.T.astype(bf16)
        if part == 2:
            val_t[...] = block.T.astype(bf16)
    per = lanes // size

    def group(g, carry):
        start = pl.multiple_of(g * lanes, lanes)
        query = qkv_ref[:, pl.ds(start, lanes)]
        keys = qkv_ref[:, pl.ds(pl.multiple_of(features + start, lanes), lanes)]
        for one in range(per):
            head = g * per + one
            at = pl.ds(pl.multiple_of(head * size, size), size)
            scores = dot_nt(keys * head_mask(one, size), query) * scaling + bias_ref[head]
            peak = jnp.max(scores, axis=0, keepdims=True)
            raised = jnp.exp(scores - peak)
            total = jnp.sum(raised, axis=0, keepdims=True)
            probs = raised * (1.0 / total)
            probs_ref[head] = probs
            mixed_t_ref[at, :] = dot_nn(val_t[at, :], probs.astype(bf16)).astype(bf16)
        return carry

    lax.fori_loop(0, heads // per, group, 0)
    mixed = mixed_t_ref[...].astype(f32).T.astype(bf16)
    mid_ref[...] = rows + dot_nn(mixed, wproj_ref[...]) + bproj_ref[...]


def mlp_fwd_kernel(
    mid_ref, gain_ref, off_ref, w1_ref, b1_ref, w2_ref, b2_ref,
    out_ref, yn_ref, slope_ref, act_ref,
):
    middle = mid_ref[...]
    features = middle.shape[1]
    unit, _ = normalize(middle)
    yn = (unit * gain_ref[...] + off_ref[...]).astype(bf16)
    yn_ref[...] = yn
    total = middle + b2_ref[...]
    for chunk in range(w1_ref.shape[1] // features):
        cols = pl.ds(chunk * features, features)
        pre = dot_nn(yn, w1_ref[:, cols]) + b1_ref[:, cols]
        cumul = 0.5 * (1.0 + lax.erf(pre * half_root))
        slope_ref[:, cols] = cumul + pre * (jnp.exp(-0.5 * pre * pre) * inv_root_tau)
        act = (pre * cumul).astype(bf16)
        act_ref[:, cols] = act
        total = total + dot_nn(act, w2_ref[cols, :])
    out_ref[...] = total


def mlp_bwd_kernel(
    g_ref, mid_ref, gain_ref, w1_ref, w2_ref, yn_ref, slope_ref, act_ref,
    gm_ref, gw1_ref, gw2_ref, gb1_ref, gb2_ref, ggain_ref, goff_ref, gbproj_ref,
):
    grad = g_ref[...]
    features = grad.shape[1]
    low = grad.astype(bf16)
    gb2_ref[...] = jnp.sum(grad, axis=0, keepdims=True)
    yn = yn_ref[...]
    g_yn = jnp.zeros_like(grad)
    for chunk in range(w1_ref.shape[1] // features):
        cols = pl.ds(chunk * features, features)
        gw2_ref[cols, :] = dot_tn(act_ref[:, cols], low).astype(bf16)
        g_pre = dot_nt(low, w2_ref[cols, :]) * slope_ref[:, cols]
        gb1_ref[:, cols] = jnp.sum(g_pre, axis=0, keepdims=True)
        pre_low = g_pre.astype(bf16)
        gw1_ref[:, cols] = dot_tn(yn, pre_low).astype(bf16)
        g_yn = g_yn + dot_nt(pre_low, w1_ref[:, cols])
    back, g_gain, g_off = norm_pull(mid_ref[...], gain_ref[...], g_yn)
    ggain_ref[...] = g_gain
    goff_ref[...] = g_off
    g_mid = grad + back
    gm_ref[...] = g_mid
    gbproj_ref[...] = jnp.sum(g_mid, axis=0, keepdims=True)


def attn_bwd_kernel(
    gm_ref, x_ref, gain_ref, wqkv_ref, wproj_ref, xn_ref, qkv_ref, key_t_ref, probs_ref,
    mixed_t_ref, spread_ref, spread_t_ref,
    gx_ref, gwqkv_ref, gwproj_ref, gqv_ref, gpairs_ref, ggain_ref, goff_ref,
    dmix, dq_t, dqkv,
):
    g_mid = gm_ref[...]
    features = g_mid.shape[1]
    heads = probs_ref.shape[0]
    size = features // heads
    scaling = size ** (-0.5)
    low = g_mid.astype(bf16)
    gwproj_ref[...] = dot_nn(mixed_t_ref[...], low).astype(bf16)
    dmix[...] = dot_nt(low, wproj_ref[...]).astype(bf16)
    per = lanes // size

    def group(g, carry):
        start = pl.multiple_of(g * lanes, lanes)
        k_at = pl.multiple_of(features + start, lanes)
        v_at = pl.multiple_of(2 * features + start, lanes)
        query = qkv_ref[:, pl.ds(start, lanes)]
        values = qkv_ref[:, pl.ds(v_at, lanes)]
        d_mix = dmix[:, pl.ds(start, lanes)]
        d_keys = jnp.zeros(query.shape, f32)
        d_values = jnp.zeros(query.shape, f32)
        for one in range(per):
            head = g * per + one
            at = pl.ds(pl.multiple_of(head * size, size), size)
            keep = head_mask(one, size)
            probs = probs_ref[head]
            d_probs = dot_nt(values * keep, d_mix)
            d_values = d_values + dot_nn(probs.astype(bf16), d_mix * keep)
            weighed = probs * d_probs
            d_scores = weighed - probs * jnp.sum(weighed, axis=0, keepdims=True)
            scores_low = d_scores.astype(bf16)
            d_keys = d_keys + dot_nn(scores_low, query * keep)
            dq_t[at, :] = dot_nn(key_t_ref[at, :], scores_low)
            folded = dot_nn(spread_t_ref[...], scores_low).astype(bf16)
            gpairs_ref[head] = dot_nn(folded, spread_ref[...])
        dqkv[:, pl.ds(k_at, lanes)] = (d_keys * scaling).astype(bf16)
        dqkv[:, pl.ds(v_at, lanes)] = d_values.astype(bf16)
        gqv_ref[1:2, pl.ds(start, lanes)] = jnp.sum(d_values, axis=0, keepdims=True)
        return carry

    lax.fori_loop(0, heads // per, group, 0)
    d_query = dq_t[...].T * scaling
    gqv_ref[0:1, :] = jnp.sum(d_query, axis=0, keepdims=True)
    dqkv[:, :features] = d_query.astype(bf16)
    xn = xn_ref[...]
    g_xn = jnp.zeros_like(g_mid)
    for part in range(3):
        cols = pl.ds(part * features, features)
        block = dqkv[:, cols]
        gwqkv_ref[:, cols] = dot_tn(xn, block).astype(bf16)
        g_xn = g_xn + dot_nt(block, wqkv_ref[:, cols])
    back, g_gain, g_off = norm_pull(x_ref[...], gain_ref[...], g_xn)
    ggain_ref[...] = g_gain
    goff_ref[...] = g_off
    gx_ref[...] = g_mid + back


def run(kernel, outs, args, scratch=(), flops=0):
    size = sum(a.size * a.dtype.itemsize for a in args)
    size += sum(a.size * a.dtype.itemsize for a in outs)
    return pl.pallas_call(
        kernel,
        out_shape=tuple(outs),
        in_specs=[pl.BlockSpec(memory_space=pltpu.VMEM)] * len(args),
        out_specs=tuple([pl.BlockSpec(memory_space=pltpu.VMEM)] * len(outs)),
        scratch_shapes=list(scratch),
        compiler_params=pltpu.CompilerParams(vmem_limit_bytes=60 * 1024 * 1024),
        cost_estimate=pl.CostEstimate(flops=flops, bytes_accessed=size, transcendentals=0),
    )(*args)


def shaped(shape, dtype):
    return jax.ShapeDtypeStruct(tuple(shape), dtype)


def offset_onehot(table_rows):
    places = jnp.arange(WIN * WIN, dtype=jnp.int32)
    row_at = places // WIN
    col_at = places % WIN
    index = (row_at[:, None] - row_at[None, :] + WIN - 1) * (2 * WIN - 1) + (
        col_at[:, None] - col_at[None, :] + WIN - 1
    )
    targets = jnp.arange(table_rows, dtype=jnp.int32)
    return (index.reshape(-1)[:, None] == targets[None, :]).astype(f32)


def token_places(shift_by):
    token = jnp.arange(SIDE * SIDE, dtype=jnp.int32)
    row = (token // SIDE - shift_by) % SIDE
    col = (token % SIDE - shift_by) % SIDE
    window = (row // WIN) * (SIDE // WIN) + col // WIN
    inside = (row % WIN) * WIN + col % WIN
    if shift_by:
        edges = SIDE - WIN, SIDE - shift_by
        a_row = (row >= edges[0]).astype(jnp.int32) + (row >= edges[1]).astype(jnp.int32)
        a_col = (col >= edges[0]).astype(jnp.int32) + (col >= edges[1]).astype(jnp.int32)
        label = 3 * a_row + a_col
    else:
        label = jnp.zeros_like(token)
    mask = jnp.where(label[:, None] == label[None, :], 0.0, mask_fill)
    mask = jnp.where(window[:, None] == window[None, :], mask, outside_fill).astype(f32)
    spread = (inside[:, None] == jnp.arange(WIN * WIN)[None, :]).astype(bf16)
    return mask, spread, spread.T


def local(
    images,
    cotangent,
    counts,
    *shards,
):
    devices = lax.axis_size("fsdp")
    gather_dims = (1, 1, 1, 2, 1, 1, 1, 1, 1, 1, 1, 1, 1)
    large_at = (2, 5, 9, 11)
    small_at = (0, 1, 3, 4, 6, 7, 8, 10, 12)
    flats = [tensor.reshape(-1) for tensor in shards]
    packed = jnp.concatenate([flats[n] for n in small_at])
    packed = lax.all_gather(packed, "fsdp", axis=0, tiled=False)
    weights = [None] * len(shards)
    at = 0
    for n in small_at:
        shape, axis_dim = shards[n].shape, gather_dims[n]
        size = flats[n].shape[0]
        piece = packed[:, at : at + size].reshape((devices,) + shape)
        piece = jnp.moveaxis(piece, 0, axis_dim)
        full = shape[:axis_dim] + (devices * shape[axis_dim],) + shape[axis_dim + 1 :]
        weights[n] = piece.reshape(full)
        at += size
    for n in large_at:
        weights[n] = [None] * LAYERS
    for layer in range(LAYERS):
        for n in large_at:
            weights[n][layer] = lax.all_gather(shards[n][layer], "fsdp", axis=0, tiled=True)
    tokens, features = images.shape[1:]
    table = weights[4]
    heads = table.shape[-1]
    hidden = weights[10].shape[-1]
    cells = WIN * WIN
    onehot = offset_onehot(table.shape[1])
    pairs = jnp.einsum("pt,lth->lhp", onehot.astype(bf16), table, preferred_element_type=f32)
    pairs = pairs.reshape(LAYERS, heads, cells, cells).transpose(0, 1, 3, 2).astype(bf16)
    zero = jnp.zeros((features,), f32)

    def row(n, layer):
        return weights[n][layer].astype(f32).reshape(1, -1)

    active = counts[0] > 0
    current = images[0].astype(f32)
    saved = []
    for layer in range(LAYERS):
        mask, spread, spread_t = token_places(SHIFT if layer % 2 else 0)
        bias = run(
            bias_kernel,
            [shaped((heads, tokens, tokens), f32)],
            (pairs[layer], spread, spread_t, mask),
        )[0]
        b_qv = weights[3][layer].astype(f32)
        b_qkv = jnp.concatenate([b_qv[0], zero, b_qv[1]]).reshape(1, -1)
        attn = run(
            attn_fwd_kernel,
            [
                shaped((tokens, features), f32),
                shaped((tokens, features), bf16),
                shaped((tokens, 3 * features), bf16),
                shaped((features, tokens), bf16),
                shaped((heads, tokens, tokens), f32),
                shaped((features, tokens), bf16),
            ],
            (current, row(0, layer), row(1, layer), weights[2][layer], b_qkv, bias,
             weights[5][layer], row(6, layer)),
            [pltpu.VMEM((features, tokens), bf16)],
        )
        mlp = run(
            mlp_fwd_kernel,
            [
                shaped((tokens, features), f32),
                shaped((tokens, features), bf16),
                shaped((tokens, hidden), f32),
                shaped((tokens, hidden), bf16),
            ],
            (attn[0], row(7, layer), row(8, layer), weights[9][layer], row(10, layer),
             weights[11][layer], row(12, layer)),
        )
        saved.append((current, attn, mlp, spread, spread_t))
        current = mlp[0]
    outs = jnp.where(active, current, 0.0)[None]
    grad = jnp.where(active, cotangent[0].astype(f32), 0.0)
    sums = [[None] * LAYERS for _ in shards]
    owned = [[None] * LAYERS for _ in shards]

    def scatter(value):
        return lax.psum_scatter(value, "fsdp", scatter_dimension=0, tiled=True).astype(f32)

    for layer in reversed(range(LAYERS)):
        entry, attn, mlp, spread, spread_t = saved[layer]
        g_mid, g_w1, g_w2, *rest = run(
            mlp_bwd_kernel,
            [
                shaped((tokens, features), f32),
                shaped((features, hidden), bf16),
                shaped((hidden, features), bf16),
                shaped((1, hidden), f32),
                shaped((1, features), f32),
                shaped((1, features), f32),
                shaped((1, features), f32),
                shaped((1, features), f32),
            ],
            (grad, attn[0], row(7, layer), weights[9][layer], weights[11][layer], *mlp[1:]),
        )
        sums[10][layer], sums[12][layer], sums[7][layer], sums[8][layer], sums[6][layer] = rest
        owned[11][layer] = scatter(g_w2)
        owned[9][layer] = scatter(g_w1)
        grad, g_qkv, g_proj, g_qv, g_pairs, g_gain, g_off = run(
            attn_bwd_kernel,
            [
                shaped((tokens, features), f32),
                shaped((features, 3 * features), bf16),
                shaped((features, features), bf16),
                shaped((2, features), f32),
                shaped((heads, cells, cells), f32),
                shaped((1, features), f32),
                shaped((1, features), f32),
            ],
            (g_mid, entry, row(0, layer), weights[2][layer], weights[5][layer], *attn[1:],
             spread, spread_t),
            [
                pltpu.VMEM((tokens, features), bf16),
                pltpu.VMEM((features, tokens), f32),
                pltpu.VMEM((tokens, 3 * features), bf16),
            ],
        )
        owned[5][layer] = scatter(g_proj)
        owned[2][layer] = scatter(g_qkv)
        sums[0][layer], sums[1][layer], sums[3][layer] = g_gain, g_off, g_qv
        per_pair = g_pairs.transpose(0, 2, 1).reshape(heads, cells * cells)
        sums[4][layer] = jnp.dot(per_pair, onehot, precision=lax.Precision.HIGHEST).T
    parts = []
    for n in small_at:
        shape, axis_dim = shards[n].shape, gather_dims[n]
        both = jnp.stack(sums[n])
        both = both.reshape(shape[:axis_dim] + (devices,) + shape[axis_dim:])
        parts.append(jnp.moveaxis(both, axis_dim, 0).reshape(devices, -1))
    summed = lax.psum_scatter(
        jnp.concatenate(parts, axis=1), "fsdp", scatter_dimension=0, tiled=False
    )
    at = 0
    for n in small_at:
        size = flats[n].shape[0]
        owned[n] = summed[at : at + size].reshape(shards[n].shape)
        at += size
    for n in large_at:
        owned[n] = jnp.stack(owned[n])
    return (outs, grad[None], *owned)


def solution(mesh):
    in_specs = (
        P("fsdp", None, None),
        P("fsdp", None, None),
        P("fsdp"),
        P(None, "fsdp"),
        P(None, "fsdp"),
        P(None, "fsdp", None),
        P(None, None, "fsdp"),
        P(None, "fsdp", None),
        P(None, "fsdp", None),
        P(None, "fsdp"),
        P(None, "fsdp"),
        P(None, "fsdp"),
        P(None, "fsdp", None),
        P(None, "fsdp"),
        P(None, "fsdp", None),
        P(None, "fsdp"),
    )
    out_specs = (
        P("fsdp", None, None),
        P("fsdp", None, None),
        P(None, "fsdp"),
        P(None, "fsdp"),
        P(None, "fsdp", None),
        P(None, None, "fsdp"),
        P(None, "fsdp", None),
        P(None, "fsdp", None),
        P(None, "fsdp"),
        P(None, "fsdp"),
        P(None, "fsdp"),
        P(None, "fsdp", None),
        P(None, "fsdp"),
        P(None, "fsdp", None),
        P(None, "fsdp"),
    )
    return jax.shard_map(local, mesh=mesh, in_specs=in_specs, out_specs=out_specs, check_vma=False)
```

```python
import functools

import jax
import jax.numpy as jnp
from jax import lax
from jax.experimental import pallas as pl
from jax.experimental.pallas import tpu as pltpu
from jax.sharding import PartitionSpec as P

WIN = 7
SIDE = 14
LAYERS = 2
SHIFT = 3

norm_eps = 1e-05
mask_fill = -10000.0
outside_fill = -1e30
half_root = 0.7071067811865476
inv_root_tau = 0.3989422804014327
lanes = 128
bf16 = jnp.bfloat16
f32 = jnp.float32


def dot_nn(left, right):
    return lax.dot_general(left, right, (((1,), (0,)), ((), ())), preferred_element_type=f32)


def dot_nt(left, right):
    return lax.dot_general(left, right, (((1,), (1,)), ((), ())), preferred_element_type=f32)


def dot_tn(left, right):
    return lax.dot_general(left, right, (((0,), (0,)), ((), ())), preferred_element_type=f32)


def normalize(rows):
    centred = rows - jnp.mean(rows, axis=-1, keepdims=True)
    spread = jnp.mean(centred * centred, axis=-1, keepdims=True)
    inverse = lax.rsqrt(spread + norm_eps)
    return centred * inverse, inverse


def norm_pull(rows, gain, grad):
    unit, inverse = normalize(rows)
    g_gain = jnp.sum(grad * unit, axis=0, keepdims=True)
    g_bias = jnp.sum(grad, axis=0, keepdims=True)
    scaled = grad * gain
    back = inverse * (
        scaled
        - jnp.mean(scaled, axis=-1, keepdims=True)
        - unit * jnp.mean(scaled * unit, axis=-1, keepdims=True)
    )
    return back, g_gain, g_bias


def head_mask(local_head, head_size):
    lane = lax.broadcasted_iota(jnp.int32, (1, lanes), 1)
    return jnp.where(lane // head_size == local_head, 1.0, 0.0).astype(bf16)


def bias_kernel(pairs_ref, spread_ref, spread_t_ref, mask_ref, out_ref):
    def step(head, carry):
        rows = dot_nn(spread_ref[...], pairs_ref[head]).astype(bf16)
        out_ref[head] = dot_nn(rows, spread_t_ref[...]) + mask_ref[...]
        return carry

    lax.fori_loop(0, pairs_ref.shape[0], step, 0)


def attn_fwd_kernel(
    x_ref, gain_ref, off_ref, wqkv_ref, bqkv_ref, bias_ref, wproj_ref, bproj_ref,
    mid_ref, xn_ref, qkv_ref, key_t_ref, probs_ref, mixed_t_ref,
    val_t,
):
    rows = x_ref[...]
    features = rows.shape[1]
    heads = bias_ref.shape[0]
    size = features // heads
    scaling = size ** (-0.5)
    unit, _ = normalize(rows)
    xn = (unit * gain_ref[...] + off_ref[...]).astype(bf16)
    xn_ref[...] = xn
    for part in range(3):
        cols = pl.ds(part * features, features)
        block = dot_nn(xn, wqkv_ref[:, cols]) + bqkv_ref[:, cols]
        qkv_ref[:, cols] = block.astype(bf16)
        if part == 1:
            key_t_ref[...] = block.T.astype(bf16)
        if part == 2:
            val_t[...] = block.T.astype(bf16)
    per = lanes // size

    def group(g, carry):
        start = pl.multiple_of(g * lanes, lanes)
        query = qkv_ref[:, pl.ds(start, lanes)]
        keys = qkv_ref[:, pl.ds(pl.multiple_of(features + start, lanes), lanes)]
        for one in range(per):
            head = g * per + one
            at = pl.ds(pl.multiple_of(head * size, size), size)
            scores = dot_nt(keys * head_mask(one, size), query) * scaling + bias_ref[head]
            peak = jnp.max(scores, axis=0, keepdims=True)
            raised = jnp.exp(scores - peak)
            total = jnp.sum(raised, axis=0, keepdims=True)
            probs = raised * (1.0 / total)
            probs_ref[head] = probs
            mixed_t_ref[at, :] = dot_nn(val_t[at, :], probs.astype(bf16)).astype(bf16)
        return carry

    lax.fori_loop(0, heads // per, group, 0)
    mixed = mixed_t_ref[...].astype(f32).T.astype(bf16)
    mid_ref[...] = rows + dot_nn(mixed, wproj_ref[...]) + bproj_ref[...]


def mlp_fwd_kernel(
    mid_ref, gain_ref, off_ref, w1_ref, b1_ref, w2_ref, b2_ref,
    out_ref, yn_ref, slope_ref, act_ref,
):
    middle = mid_ref[...]
    features = middle.shape[1]
    unit, _ = normalize(middle)
    yn = (unit * gain_ref[...] + off_ref[...]).astype(bf16)
    yn_ref[...] = yn
    total = middle + b2_ref[...]
    for chunk in range(w1_ref.shape[1] // features):
        cols = pl.ds(chunk * features, features)
        pre = dot_nn(yn, w1_ref[:, cols]) + b1_ref[:, cols]
        cumul = 0.5 * (1.0 + lax.erf(pre * half_root))
        slope_ref[:, cols] = cumul + pre * (jnp.exp(-0.5 * pre * pre) * inv_root_tau)
        act = (pre * cumul).astype(bf16)
        act_ref[:, cols] = act
        total = total + dot_nn(act, w2_ref[cols, :])
    out_ref[...] = total


def mlp_bwd_kernel(
    g_ref, mid_ref, gain_ref, w1_ref, w2_ref, yn_ref, slope_ref, act_ref,
    gm_ref, gw1_ref, gw2_ref, gb1_ref, gb2_ref, ggain_ref, goff_ref, gbproj_ref,
):
    grad = g_ref[...]
    features = grad.shape[1]
    low = grad.astype(bf16)
    gb2_ref[...] = jnp.sum(grad, axis=0, keepdims=True)
    yn = yn_ref[...]
    g_yn = jnp.zeros_like(grad)
    for chunk in range(w1_ref.shape[1] // features):
        cols = pl.ds(chunk * features, features)
        gw2_ref[cols, :] = dot_tn(act_ref[:, cols], low).astype(bf16)
        g_pre = dot_nt(low, w2_ref[cols, :]) * slope_ref[:, cols]
        gb1_ref[:, cols] = jnp.sum(g_pre, axis=0, keepdims=True)
        pre_low = g_pre.astype(bf16)
        gw1_ref[:, cols] = dot_tn(yn, pre_low).astype(bf16)
        g_yn = g_yn + dot_nt(pre_low, w1_ref[:, cols])
    back, g_gain, g_off = norm_pull(mid_ref[...], gain_ref[...], g_yn)
    ggain_ref[...] = g_gain
    goff_ref[...] = g_off
    g_mid = grad + back
    gm_ref[...] = g_mid
    gbproj_ref[...] = jnp.sum(g_mid, axis=0, keepdims=True)


def attn_bwd_kernel(
    gm_ref, x_ref, gain_ref, wqkv_ref, wproj_ref, xn_ref, qkv_ref, key_t_ref, probs_ref,
    mixed_t_ref, spread_ref, spread_t_ref,
    gx_ref, gwqkv_ref, gwproj_ref, gqv_ref, gpairs_ref, ggain_ref, goff_ref,
    dmix, dq_t, dqkv,
):
    g_mid = gm_ref[...]
    features = g_mid.shape[1]
    heads = probs_ref.shape[0]
    size = features // heads
    scaling = size ** (-0.5)
    low = g_mid.astype(bf16)
    gwproj_ref[...] = dot_nn(mixed_t_ref[...], low).astype(bf16)
    dmix[...] = dot_nt(low, wproj_ref[...]).astype(bf16)
    per = lanes // size

    def group(g, carry):
        start = pl.multiple_of(g * lanes, lanes)
        k_at = pl.multiple_of(features + start, lanes)
        v_at = pl.multiple_of(2 * features + start, lanes)
        query = qkv_ref[:, pl.ds(start, lanes)]
        values = qkv_ref[:, pl.ds(v_at, lanes)]
        d_mix = dmix[:, pl.ds(start, lanes)]
        d_keys = jnp.zeros(query.shape, f32)
        d_values = jnp.zeros(query.shape, f32)
        for one in range(per):
            head = g * per + one
            at = pl.ds(pl.multiple_of(head * size, size), size)
            keep = head_mask(one, size)
            probs = probs_ref[head]
            d_probs = dot_nt(values * keep, d_mix)
            d_values = d_values + dot_nn(probs.astype(bf16), d_mix * keep)
            weighed = probs * d_probs
            d_scores = weighed - probs * jnp.sum(weighed, axis=0, keepdims=True)
            scores_low = d_scores.astype(bf16)
            d_keys = d_keys + dot_nn(scores_low, query * keep)
            dq_t[at, :] = dot_nn(key_t_ref[at, :], scores_low)
            folded = dot_nn(spread_t_ref[...], scores_low).astype(bf16)
            gpairs_ref[head] = dot_nn(folded, spread_ref[...])
        dqkv[:, pl.ds(k_at, lanes)] = (d_keys * scaling).astype(bf16)
        dqkv[:, pl.ds(v_at, lanes)] = d_values.astype(bf16)
        gqv_ref[1:2, pl.ds(start, lanes)] = jnp.sum(d_values, axis=0, keepdims=True)
        return carry

    lax.fori_loop(0, heads // per, group, 0)
    d_query = dq_t[...].T * scaling
    gqv_ref[0:1, :] = jnp.sum(d_query, axis=0, keepdims=True)
    dqkv[:, :features] = d_query.astype(bf16)
    xn = xn_ref[...]
    g_xn = jnp.zeros_like(g_mid)
    for part in range(3):
        cols = pl.ds(part * features, features)
        block = dqkv[:, cols]
        gwqkv_ref[:, cols] = dot_tn(xn, block).astype(bf16)
        g_xn = g_xn + dot_nt(block, wqkv_ref[:, cols])
    back, g_gain, g_off = norm_pull(x_ref[...], gain_ref[...], g_xn)
    ggain_ref[...] = g_gain
    goff_ref[...] = g_off
    gx_ref[...] = g_mid + back


def bit_of(index, place):
    return lax.rem(index // (1 << place), 2)


def peers_of(me, places):
    return [me + (1 - 2 * bit_of(me, place)) * (1 << place) for place in range(places)]


def greet(me, places):
    barrier = pltpu.get_barrier_semaphore()
    for peer in peers_of(me, places):
        pl.semaphore_signal(
            barrier, inc=1, device_id=(peer,), device_id_type=pl.DeviceIdType.MESH
        )
    pl.semaphore_wait(barrier, places)


def routes(places):
    high = list(range(places - 1, 2, -1))
    if places < 3:
        return [list(range(places - 1, -1, -1))]
    return [
        high + [2, 1, 0],
        high + [1, 2, 0],
        [2] + high + [1, 0],
        [1] + high + [2, 0],
    ]


def row_parts(total, count):
    units = total // 16
    sizes = [16 * (units // count + (1 if n < units % count else 0)) for n in range(count)]
    return [(sum(sizes[:n]), sizes[n]) for n in range(count)]


def region(places, free, me, lowest=0, forced=None):
    picks = []
    for place in range(places - 1, lowest - 1, -1):
        if forced is not None and place == forced[0]:
            picks.append(forced[1])
        elif place in free:
            picks.append(slice(None))
        else:
            picks.append(bit_of(me, place))
    return tuple(picks)


def gather_kernel(places, x_ref, out_ref, send_sem, recv_sem, own_sem):
    me = lax.axis_index("fsdp")
    peers = peers_of(me, places)
    greet(me, places)
    own = pltpu.make_async_copy(x_ref, out_ref.at[region(places, (), me)], own_sem)
    own.start()
    orders = routes(places)
    parts = row_parts(x_ref.shape[0], len(orders))
    copies = [[] for _ in orders]
    for stage in range(places):
        for n, (order, (low, size)) in enumerate(zip(orders, parts)):
            rows = pl.ds(low, size)
            place = order[stage]
            if stage == 1 and n == 0:
                own.wait()
            if stage:
                copies[n][-1].wait_recv()
            here = region(places, order[:stage], me)
            target = out_ref.at[here + (rows,)]
            copy = pltpu.make_async_remote_copy(
                src_ref=x_ref.at[rows] if stage == 0 else target,
                dst_ref=target,
                send_sem=send_sem.at[n, stage],
                recv_sem=recv_sem.at[n, stage],
                device_id=(peers[place],),
                device_id_type=pl.DeviceIdType.MESH,
            )
            copy.start()
            copies[n].append(copy)
    for group in copies:
        group[-1].wait_recv()
    for group in copies:
        for copy in group:
            copy.wait_send()


def scatter_kernel(places, g_ref, out_ref, acc, *rest):
    landings, (send_sem, recv_sem) = rest[:places], rest[places:]
    me = lax.axis_index("fsdp")
    peers = peers_of(me, places)
    greet(me, places)
    orders = [order[::-1] for order in routes(places)]
    parts = row_parts(g_ref.shape[-2], len(orders))
    everything = set(range(places))
    copies = [[None] * places for _ in orders]

    def send(n, stage):
        order, (low, size) = orders[n], parts[n]
        rows = pl.ds(low, size)
        place = order[stage]
        free = everything - set(order[: stage + 1])
        away = (place, 1 - bit_of(me, place))
        if stage == 0:
            source = g_ref.at[region(places, free, me, 0, away) + (rows,)]
        else:
            source = acc.at[region(places, free, me, 1, away) + (rows,)]
        copy = pltpu.make_async_remote_copy(
            src_ref=source,
            dst_ref=landings[stage].at[(slice(None),) * len(free) + (rows,)],
            send_sem=send_sem.at[n, stage],
            recv_sem=recv_sem.at[n, stage],
            device_id=(peers[place],),
            device_id_type=pl.DeviceIdType.MESH,
        )
        copy.start()
        copies[n][stage] = copy

    def add(n, stage):
        order, (low, size) = orders[n], parts[n]
        rows = pl.ds(low, size)
        free = sorted(everything - set(order[: stage + 1]), reverse=True)
        copies[n][stage].wait_recv()

        def one(at, carry):
            values = {}
            for spot, place in enumerate(free):
                values[place] = lax.rem(at // (1 << (len(free) - 1 - spot)), 2)
            full = tuple(
                values[place] if place in values else bit_of(me, place)
                for place in range(places - 1, -1, -1)
            )
            kept = full[:-1] + (rows,)
            landed = landings[stage][tuple(values[place] for place in free) + (rows,)]
            if stage == 0:
                acc[kept] = g_ref[full + (rows,)] + landed
            elif stage < places - 1:
                acc[kept] = acc[kept] + landed
            else:
                out_ref[rows] = acc[kept].astype(f32) + landed.astype(f32)
            return carry

        lax.fori_loop(0, 1 << len(free), one, 0)

    for n in range(len(orders)):
        send(n, 0)
    for stage in range(places):
        for n in range(len(orders)):
            add(n, stage)
            if stage < places - 1:
                send(n, stage + 1)
    for group in copies:
        for copy in group:
            copy.wait_send()


def gather_all(shard, devices):
    places = devices.bit_length() - 1
    count = len(routes(places))
    out = pl.pallas_call(
        functools.partial(gather_kernel, places),
        out_shape=shaped((2,) * places + shard.shape, shard.dtype),
        in_specs=[pl.BlockSpec(memory_space=pltpu.VMEM)],
        out_specs=pl.BlockSpec(memory_space=pltpu.VMEM),
        scratch_shapes=[
            pltpu.SemaphoreType.DMA((count, places)),
            pltpu.SemaphoreType.DMA((count, places)),
            pltpu.SemaphoreType.DMA,
        ],
        compiler_params=pltpu.CompilerParams(
            collective_id=0, has_side_effects=True, vmem_limit_bytes=60 * 1024 * 1024
        ),
    )(shard)
    return out.reshape((devices,) + shard.shape)


def scatter_all(grads, devices):
    places = devices.bit_length() - 1
    count = len(routes(places))
    tail = grads.shape[1:]
    return pl.pallas_call(
        functools.partial(scatter_kernel, places),
        out_shape=shaped(tail, f32),
        in_specs=[pl.BlockSpec(memory_space=pltpu.VMEM)],
        out_specs=pl.BlockSpec(memory_space=pltpu.VMEM),
        scratch_shapes=[pltpu.VMEM((2,) * (places - 1) + tail, bf16)]
        + [pltpu.VMEM((2,) * (places - 1 - stage) + tail, bf16) for stage in range(places)]
        + [
            pltpu.SemaphoreType.DMA((count, places)),
            pltpu.SemaphoreType.DMA((count, places)),
        ],
        compiler_params=pltpu.CompilerParams(
            collective_id=1, has_side_effects=True, vmem_limit_bytes=60 * 1024 * 1024
        ),
    )(grads.reshape((2,) * places + tail))


def run(kernel, outs, args, scratch=(), flops=0):
    size = sum(a.size * a.dtype.itemsize for a in args)
    size += sum(a.size * a.dtype.itemsize for a in outs)
    return pl.pallas_call(
        kernel,
        out_shape=tuple(outs),
        in_specs=[pl.BlockSpec(memory_space=pltpu.VMEM)] * len(args),
        out_specs=tuple([pl.BlockSpec(memory_space=pltpu.VMEM)] * len(outs)),
        scratch_shapes=list(scratch),
        compiler_params=pltpu.CompilerParams(vmem_limit_bytes=60 * 1024 * 1024),
        cost_estimate=pl.CostEstimate(flops=flops, bytes_accessed=size, transcendentals=0),
    )(*args)


def shaped(shape, dtype):
    return jax.ShapeDtypeStruct(tuple(shape), dtype)


def offset_onehot(table_rows):
    places = jnp.arange(WIN * WIN, dtype=jnp.int32)
    row_at = places // WIN
    col_at = places % WIN
    index = (row_at[:, None] - row_at[None, :] + WIN - 1) * (2 * WIN - 1) + (
        col_at[:, None] - col_at[None, :] + WIN - 1
    )
    targets = jnp.arange(table_rows, dtype=jnp.int32)
    return (index.reshape(-1)[:, None] == targets[None, :]).astype(f32)


def token_places(shift_by):
    token = jnp.arange(SIDE * SIDE, dtype=jnp.int32)
    row = (token // SIDE - shift_by) % SIDE
    col = (token % SIDE - shift_by) % SIDE
    window = (row // WIN) * (SIDE // WIN) + col // WIN
    inside = (row % WIN) * WIN + col % WIN
    if shift_by:
        edges = SIDE - WIN, SIDE - shift_by
        a_row = (row >= edges[0]).astype(jnp.int32) + (row >= edges[1]).astype(jnp.int32)
        a_col = (col >= edges[0]).astype(jnp.int32) + (col >= edges[1]).astype(jnp.int32)
        label = 3 * a_row + a_col
    else:
        label = jnp.zeros_like(token)
    mask = jnp.where(label[:, None] == label[None, :], 0.0, mask_fill)
    mask = jnp.where(window[:, None] == window[None, :], mask, outside_fill).astype(f32)
    spread = (inside[:, None] == jnp.arange(WIN * WIN)[None, :]).astype(bf16)
    return mask, spread, spread.T


def local(
    images,
    cotangent,
    counts,
    *shards,
):
    devices = lax.axis_size("fsdp")
    gather_dims = (1, 1, 1, 2, 1, 1, 1, 1, 1, 1, 1, 1, 1)
    large_at = (2, 5, 9, 11)
    small_at = (0, 1, 3, 4, 6, 7, 8, 10, 12)
    flats = [tensor.reshape(-1) for tensor in shards]
    tokens, features = images.shape[1:]
    packed = jnp.concatenate([flats[n] for n in small_at])
    small_rows = 16 * -(-packed.shape[0] // (16 * features))
    packed = jnp.pad(packed, (0, small_rows * features - packed.shape[0]))
    blocks, spans = [packed.reshape(small_rows, features)], {}
    filled = small_rows
    for layer in range(LAYERS):
        for n in large_at:
            piece = shards[n][layer]
            rows, wide = piece.shape[0], piece.shape[1] // features
            piece = piece.reshape(rows, wide, features).transpose(1, 0, 2)
            blocks.append(piece.reshape(rows * wide, features))
            spans[n, layer] = (filled, rows, wide)
            filled += rows * wide
    spare = -filled % 16
    if spare:
        blocks.append(jnp.zeros((spare, features), bf16))
    gathered = gather_all(jnp.concatenate(blocks), devices)
    packed = gathered[:, :small_rows].reshape(devices, -1)
    weights = [None] * len(shards)
    at = 0
    for n in small_at:
        shape, axis_dim = shards[n].shape, gather_dims[n]
        size = flats[n].shape[0]
        piece = packed[:, at : at + size].reshape((devices,) + shape)
        piece = jnp.moveaxis(piece, 0, axis_dim)
        full = shape[:axis_dim] + (devices * shape[axis_dim],) + shape[axis_dim + 1 :]
        weights[n] = piece.reshape(full)
        at += size
    for n in large_at:
        weights[n] = [None] * LAYERS
        for layer in range(LAYERS):
            low, rows, wide = spans[n, layer]
            piece = gathered[:, low : low + rows * wide]
            piece = piece.reshape(devices, wide, rows, features).transpose(0, 2, 1, 3)
            weights[n][layer] = piece.reshape(devices * rows, wide * features)
    table = weights[4]
    heads = table.shape[-1]
    hidden = weights[10].shape[-1]
    cells = WIN * WIN
    onehot = offset_onehot(table.shape[1])
    pairs = jnp.einsum("pt,lth->lhp", onehot.astype(bf16), table, preferred_element_type=f32)
    pairs = pairs.reshape(LAYERS, heads, cells, cells).transpose(0, 1, 3, 2).astype(bf16)
    zero = jnp.zeros((features,), f32)

    def row(n, layer):
        return weights[n][layer].astype(f32).reshape(1, -1)

    active = counts[0] > 0
    current = images[0].astype(f32)
    saved = []
    for layer in range(LAYERS):
        mask, spread, spread_t = token_places(SHIFT if layer % 2 else 0)
        bias = run(
            bias_kernel,
            [shaped((heads, tokens, tokens), f32)],
            (pairs[layer], spread, spread_t, mask),
        )[0]
        b_qv = weights[3][layer].astype(f32)
        b_qkv = jnp.concatenate([b_qv[0], zero, b_qv[1]]).reshape(1, -1)
        attn = run(
            attn_fwd_kernel,
            [
                shaped((tokens, features), f32),
                shaped((tokens, features), bf16),
                shaped((tokens, 3 * features), bf16),
                shaped((features, tokens), bf16),
                shaped((heads, tokens, tokens), f32),
                shaped((features, tokens), bf16),
            ],
            (current, row(0, layer), row(1, layer), weights[2][layer], b_qkv, bias,
             weights[5][layer], row(6, layer)),
            [pltpu.VMEM((features, tokens), bf16)],
        )
        mlp = run(
            mlp_fwd_kernel,
            [
                shaped((tokens, features), f32),
                shaped((tokens, features), bf16),
                shaped((tokens, hidden), f32),
                shaped((tokens, hidden), bf16),
            ],
            (attn[0], row(7, layer), row(8, layer), weights[9][layer], row(10, layer),
             weights[11][layer], row(12, layer)),
        )
        saved.append((current, attn, mlp, spread, spread_t))
        current = mlp[0]
    outs = jnp.where(active, current, 0.0)[None]
    grad = jnp.where(active, cotangent[0].astype(f32), 0.0)
    sums = [[None] * LAYERS for _ in shards]
    owned = [[None] * LAYERS for _ in shards]

    def scatter(value):
        return value

    for layer in reversed(range(LAYERS)):
        entry, attn, mlp, spread, spread_t = saved[layer]
        g_mid, g_w1, g_w2, *rest = run(
            mlp_bwd_kernel,
            [
                shaped((tokens, features), f32),
                shaped((features, hidden), bf16),
                shaped((hidden, features), bf16),
                shaped((1, hidden), f32),
                shaped((1, features), f32),
                shaped((1, features), f32),
                shaped((1, features), f32),
                shaped((1, features), f32),
            ],
            (grad, attn[0], row(7, layer), weights[9][layer], weights[11][layer], *mlp[1:]),
        )
        sums[10][layer], sums[12][layer], sums[7][layer], sums[8][layer], sums[6][layer] = rest
        owned[11][layer] = scatter(g_w2)
        owned[9][layer] = scatter(g_w1)
        grad, g_qkv, g_proj, g_qv, g_pairs, g_gain, g_off = run(
            attn_bwd_kernel,
            [
                shaped((tokens, features), f32),
                shaped((features, 3 * features), bf16),
                shaped((features, features), bf16),
                shaped((2, features), f32),
                shaped((heads, cells, cells), f32),
                shaped((1, features), f32),
                shaped((1, features), f32),
            ],
            (g_mid, entry, row(0, layer), weights[2][layer], weights[5][layer], *attn[1:],
             spread, spread_t),
            [
                pltpu.VMEM((tokens, features), bf16),
                pltpu.VMEM((features, tokens), f32),
                pltpu.VMEM((tokens, 3 * features), bf16),
            ],
        )
        owned[5][layer] = scatter(g_proj)
        owned[2][layer] = scatter(g_qkv)
        sums[0][layer], sums[1][layer], sums[3][layer] = g_gain, g_off, g_qv
        per_pair = g_pairs.transpose(0, 2, 1).reshape(heads, cells * cells)
        sums[4][layer] = jnp.dot(per_pair, onehot, precision=lax.Precision.HIGHEST).T
    parts = []
    for n in small_at:
        shape, axis_dim = shards[n].shape, gather_dims[n]
        both = jnp.stack(sums[n])
        both = both.reshape(shape[:axis_dim] + (devices,) + shape[axis_dim:])
        parts.append(jnp.moveaxis(both, axis_dim, 0).reshape(devices, -1))
    packed = jnp.concatenate(parts, axis=1).astype(bf16)
    packed = jnp.pad(packed, ((0, 0), (0, small_rows * features - packed.shape[1])))
    blocks = [packed.reshape(devices, small_rows, features)]
    for layer in range(LAYERS):
        for n in large_at:
            low, rows, wide = spans[n, layer]
            piece = owned[n][layer].reshape(devices, rows, wide, features)
            blocks.append(piece.transpose(0, 2, 1, 3).reshape(devices, rows * wide, features))
    if spare:
        blocks.append(jnp.zeros((devices, spare, features), bf16))
    reduced = scatter_all(jnp.concatenate(blocks, axis=1), devices)
    summed = reduced[:small_rows].reshape(-1)
    at = 0
    for n in small_at:
        size = flats[n].shape[0]
        owned[n] = summed[at : at + size].reshape(shards[n].shape)
        at += size
    for n in large_at:
        for layer in range(LAYERS):
            low, rows, wide = spans[n, layer]
            piece = reduced[low : low + rows * wide].reshape(wide, rows, features)
            owned[n][layer] = piece.transpose(1, 0, 2).reshape(rows, wide * features)
        owned[n] = jnp.stack(owned[n])
    return (outs, grad[None], *owned)


def solution(mesh):
    in_specs = (
        P("fsdp", None, None),
        P("fsdp", None, None),
        P("fsdp"),
        P(None, "fsdp"),
        P(None, "fsdp"),
        P(None, "fsdp", None),
        P(None, None, "fsdp"),
        P(None, "fsdp", None),
        P(None, "fsdp", None),
        P(None, "fsdp"),
        P(None, "fsdp"),
        P(None, "fsdp"),
        P(None, "fsdp", None),
        P(None, "fsdp"),
        P(None, "fsdp", None),
        P(None, "fsdp"),
    )
    out_specs = (
        P("fsdp", None, None),
        P("fsdp", None, None),
        P(None, "fsdp"),
        P(None, "fsdp"),
        P(None, "fsdp", None),
        P(None, None, "fsdp"),
        P(None, "fsdp", None),
        P(None, "fsdp", None),
        P(None, "fsdp"),
        P(None, "fsdp"),
        P(None, "fsdp"),
        P(None, "fsdp", None),
        P(None, "fsdp"),
        P(None, "fsdp", None),
        P(None, "fsdp"),
    )
    return jax.shard_map(local, mesh=mesh, in_specs=in_specs, out_specs=out_specs, check_vma=False)
```

```python
import functools

import jax
import jax.numpy as jnp
from jax import lax
from jax.experimental import pallas as pl
from jax.experimental.pallas import tpu as pltpu
from jax.sharding import PartitionSpec as P

WIN = 7
SIDE = 14
LAYERS = 2
SHIFT = 3

norm_eps = 1e-05
mask_fill = -10000.0
outside_fill = -1e30
half_root = 0.7071067811865476
inv_root_tau = 0.3989422804014327
lanes = 128
bf16 = jnp.bfloat16
f32 = jnp.float32


def dot_nn(left, right):
    return lax.dot_general(left, right, (((1,), (0,)), ((), ())), preferred_element_type=f32)


def dot_nt(left, right):
    return lax.dot_general(left, right, (((1,), (1,)), ((), ())), preferred_element_type=f32)


def dot_tn(left, right):
    return lax.dot_general(left, right, (((0,), (0,)), ((), ())), preferred_element_type=f32)


def normalize(rows):
    centred = rows - jnp.mean(rows, axis=-1, keepdims=True)
    spread = jnp.mean(centred * centred, axis=-1, keepdims=True)
    inverse = lax.rsqrt(spread + norm_eps)
    return centred * inverse, inverse


def norm_pull(rows, gain, grad):
    unit, inverse = normalize(rows)
    g_gain = jnp.sum(grad * unit, axis=0, keepdims=True)
    g_bias = jnp.sum(grad, axis=0, keepdims=True)
    scaled = grad * gain
    back = inverse * (
        scaled
        - jnp.mean(scaled, axis=-1, keepdims=True)
        - unit * jnp.mean(scaled * unit, axis=-1, keepdims=True)
    )
    return back, g_gain, g_bias


def head_mask(local_head, head_size):
    lane = lax.broadcasted_iota(jnp.int32, (1, lanes), 1)
    return jnp.where(lane // head_size == local_head, 1.0, 0.0).astype(bf16)


def bias_kernel(pairs_ref, spread_ref, spread_t_ref, mask_ref, out_ref):
    def step(head, carry):
        rows = dot_nn(spread_ref[...], pairs_ref[head]).astype(bf16)
        out_ref[head] = dot_nn(rows, spread_t_ref[...]) + mask_ref[...]
        return carry

    lax.fori_loop(0, pairs_ref.shape[0], step, 0)


def attn_fwd_kernel(
    x_ref, gain_ref, off_ref, wqkv_ref, bqkv_ref, bias_ref, wproj_ref, bproj_ref,
    mid_ref, xn_ref, qkv_ref, key_t_ref, probs_ref, mixed_t_ref,
    val_t,
):
    rows = x_ref[...]
    features = rows.shape[1]
    heads = bias_ref.shape[0]
    size = features // heads
    scaling = size ** (-0.5)
    unit, _ = normalize(rows)
    xn = (unit * gain_ref[...] + off_ref[...]).astype(bf16)
    xn_ref[...] = xn
    for part in range(3):
        cols = pl.ds(part * features, features)
        block = dot_nn(xn, wqkv_ref[part]) + bqkv_ref[:, cols]
        qkv_ref[:, cols] = block.astype(bf16)
        if part == 1:
            key_t_ref[...] = block.T.astype(bf16)
        if part == 2:
            val_t[...] = block.T.astype(bf16)
    per = lanes // size

    def group(g, carry):
        start = pl.multiple_of(g * lanes, lanes)
        query = qkv_ref[:, pl.ds(start, lanes)]
        keys = qkv_ref[:, pl.ds(pl.multiple_of(features + start, lanes), lanes)]
        for one in range(per):
            head = g * per + one
            at = pl.ds(pl.multiple_of(head * size, size), size)
            scores = dot_nt(keys * head_mask(one, size), query) * scaling + bias_ref[head]
            peak = jnp.max(scores, axis=0, keepdims=True)
            raised = jnp.exp(scores - peak)
            total = jnp.sum(raised, axis=0, keepdims=True)
            probs = raised * (1.0 / total)
            probs_ref[head] = probs
            mixed_t_ref[at, :] = dot_nn(val_t[at, :], probs.astype(bf16)).astype(bf16)
        return carry

    lax.fori_loop(0, heads // per, group, 0)
    mixed = mixed_t_ref[...].astype(f32).T.astype(bf16)
    mid_ref[...] = rows + dot_nn(mixed, wproj_ref[...]) + bproj_ref[...]


def mlp_fwd_kernel(
    mid_ref, gain_ref, off_ref, w1_ref, b1_ref, w2_ref, b2_ref,
    out_ref, yn_ref, slope_ref, act_ref,
):
    middle = mid_ref[...]
    features = middle.shape[1]
    unit, _ = normalize(middle)
    yn = (unit * gain_ref[...] + off_ref[...]).astype(bf16)
    yn_ref[...] = yn
    total = middle + b2_ref[...]
    for chunk in range(w1_ref.shape[0]):
        cols = pl.ds(chunk * features, features)
        pre = dot_nn(yn, w1_ref[chunk]) + b1_ref[:, cols]
        cumul = 0.5 * (1.0 + lax.erf(pre * half_root))
        slope_ref[:, cols] = cumul + pre * (jnp.exp(-0.5 * pre * pre) * inv_root_tau)
        act = (pre * cumul).astype(bf16)
        act_ref[:, cols] = act
        total = total + dot_nn(act, w2_ref[cols, :])
    out_ref[...] = total


def mlp_bwd_kernel(
    g_ref, mid_ref, gain_ref, w1_ref, w2_ref, yn_ref, slope_ref, act_ref,
    gm_ref, gw1_ref, gw2_ref, gb1_ref, gb2_ref, ggain_ref, goff_ref, gbproj_ref,
):
    grad = g_ref[...]
    features = grad.shape[1]
    low = grad.astype(bf16)
    gb2_ref[...] = jnp.sum(grad, axis=0, keepdims=True)
    yn = yn_ref[...]
    g_yn = jnp.zeros_like(grad)
    for chunk in range(w1_ref.shape[0]):
        cols = pl.ds(chunk * features, features)
        gw2_ref[cols, :] = dot_tn(act_ref[:, cols], low).astype(bf16)
        g_pre = dot_nt(low, w2_ref[cols, :]) * slope_ref[:, cols]
        gb1_ref[:, cols] = jnp.sum(g_pre, axis=0, keepdims=True)
        pre_low = g_pre.astype(bf16)
        gw1_ref[chunk] = dot_tn(yn, pre_low).astype(bf16)
        g_yn = g_yn + dot_nt(pre_low, w1_ref[chunk])
    back, g_gain, g_off = norm_pull(mid_ref[...], gain_ref[...], g_yn)
    ggain_ref[...] = g_gain
    goff_ref[...] = g_off
    g_mid = grad + back
    gm_ref[...] = g_mid
    gbproj_ref[...] = jnp.sum(g_mid, axis=0, keepdims=True)


def attn_bwd_kernel(
    gm_ref, x_ref, gain_ref, wqkv_ref, wproj_ref, xn_ref, qkv_ref, key_t_ref, probs_ref,
    mixed_t_ref, spread_ref, spread_t_ref,
    gx_ref, gwqkv_ref, gwproj_ref, gqv_ref, gpairs_ref, ggain_ref, goff_ref,
    dmix, dq_t, dqkv,
):
    g_mid = gm_ref[...]
    features = g_mid.shape[1]
    heads = probs_ref.shape[0]
    size = features // heads
    scaling = size ** (-0.5)
    low = g_mid.astype(bf16)
    gwproj_ref[...] = dot_nn(mixed_t_ref[...], low).astype(bf16)
    dmix[...] = dot_nt(low, wproj_ref[...]).astype(bf16)
    per = lanes // size

    def group(g, carry):
        start = pl.multiple_of(g * lanes, lanes)
        k_at = pl.multiple_of(features + start, lanes)
        v_at = pl.multiple_of(2 * features + start, lanes)
        query = qkv_ref[:, pl.ds(start, lanes)]
        values = qkv_ref[:, pl.ds(v_at, lanes)]
        d_mix = dmix[:, pl.ds(start, lanes)]
        d_keys = jnp.zeros(query.shape, f32)
        d_values = jnp.zeros(query.shape, f32)
        for one in range(per):
            head = g * per + one
            at = pl.ds(pl.multiple_of(head * size, size), size)
            keep = head_mask(one, size)
            probs = probs_ref[head]
            d_probs = dot_nt(values * keep, d_mix)
            d_values = d_values + dot_nn(probs.astype(bf16), d_mix * keep)
            weighed = probs * d_probs
            d_scores = weighed - probs * jnp.sum(weighed, axis=0, keepdims=True)
            scores_low = d_scores.astype(bf16)
            d_keys = d_keys + dot_nn(scores_low, query * keep)
            dq_t[at, :] = dot_nn(key_t_ref[at, :], scores_low)
            folded = dot_nn(spread_t_ref[...], scores_low).astype(bf16)
            gpairs_ref[head] = dot_nn(folded, spread_ref[...])
        dqkv[:, pl.ds(k_at, lanes)] = (d_keys * scaling).astype(bf16)
        dqkv[:, pl.ds(v_at, lanes)] = d_values.astype(bf16)
        gqv_ref[1:2, pl.ds(start, lanes)] = jnp.sum(d_values, axis=0, keepdims=True)
        return carry

    lax.fori_loop(0, heads // per, group, 0)
    d_query = dq_t[...].T * scaling
    gqv_ref[0:1, :] = jnp.sum(d_query, axis=0, keepdims=True)
    dqkv[:, :features] = d_query.astype(bf16)
    xn = xn_ref[...]
    g_xn = jnp.zeros_like(g_mid)
    for part in range(3):
        cols = pl.ds(part * features, features)
        block = dqkv[:, cols]
        gwqkv_ref[part] = dot_tn(xn, block).astype(bf16)
        g_xn = g_xn + dot_nt(block, wqkv_ref[part])
    back, g_gain, g_off = norm_pull(x_ref[...], gain_ref[...], g_xn)
    ggain_ref[...] = g_gain
    goff_ref[...] = g_off
    gx_ref[...] = g_mid + back


def bit_of(index, place):
    return lax.rem(index // (1 << place), 2)


def peers_of(me, places):
    return [me + (1 - 2 * bit_of(me, place)) * (1 << place) for place in range(places)]


def greet(me, places):
    barrier = pltpu.get_barrier_semaphore()
    for peer in peers_of(me, places):
        pl.semaphore_signal(
            barrier, inc=1, device_id=(peer,), device_id_type=pl.DeviceIdType.MESH
        )
    pl.semaphore_wait(barrier, places)


def routes(places):
    high = list(range(places - 1, 2, -1))
    if places < 3:
        return [list(range(places - 1, -1, -1))]
    return [
        high + [2, 1, 0],
        high + [1, 2, 0],
        [2] + high + [1, 0],
        [1] + high + [2, 0],
    ]


def row_parts(total, count):
    units = total // 16
    sizes = [16 * (units // count + (1 if n < units % count else 0)) for n in range(count)]
    return [(sum(sizes[:n]), sizes[n]) for n in range(count)]


def region(places, free, me, lowest=0, forced=None):
    picks = []
    for place in range(places - 1, lowest - 1, -1):
        if forced is not None and place == forced[0]:
            picks.append(forced[1])
        elif place in free:
            picks.append(slice(None))
        else:
            picks.append(bit_of(me, place))
    return tuple(picks)


def gather_kernel(places, x_ref, out_ref, send_sem, recv_sem, own_sem):
    me = lax.axis_index("fsdp")
    peers = peers_of(me, places)
    greet(me, places)
    own = pltpu.make_async_copy(x_ref, out_ref.at[region(places, (), me)], own_sem)
    own.start()
    orders = routes(places)
    parts = row_parts(x_ref.shape[0], len(orders))
    copies = [[] for _ in orders]
    for stage in range(places):
        for n, (order, (low, size)) in enumerate(zip(orders, parts)):
            rows = pl.ds(low, size)
            place = order[stage]
            if stage == 1 and n == 0:
                own.wait()
            if stage:
                copies[n][-1].wait_recv()
            here = region(places, order[:stage], me)
            target = out_ref.at[here + (rows,)]
            copy = pltpu.make_async_remote_copy(
                src_ref=x_ref.at[rows] if stage == 0 else target,
                dst_ref=target,
                send_sem=send_sem.at[n, stage],
                recv_sem=recv_sem.at[n, stage],
                device_id=(peers[place],),
                device_id_type=pl.DeviceIdType.MESH,
            )
            copy.start()
            copies[n].append(copy)
    for group in copies:
        group[-1].wait_recv()
    for group in copies:
        for copy in group:
            copy.wait_send()


def scatter_kernel(places, g_ref, out_ref, acc, *rest):
    landings, (send_sem, recv_sem) = rest[:places], rest[places:]
    me = lax.axis_index("fsdp")
    peers = peers_of(me, places)
    greet(me, places)
    orders = [order[::-1] for order in routes(places)]
    parts = row_parts(g_ref.shape[-2], len(orders))
    everything = set(range(places))
    copies = [[None] * places for _ in orders]

    def send(n, stage):
        order, (low, size) = orders[n], parts[n]
        rows = pl.ds(low, size)
        place = order[stage]
        free = everything - set(order[: stage + 1])
        away = (place, 1 - bit_of(me, place))
        if stage == 0:
            source = g_ref.at[region(places, free, me, 0, away) + (rows,)]
        else:
            source = acc.at[region(places, free, me, 1, away) + (rows,)]
        copy = pltpu.make_async_remote_copy(
            src_ref=source,
            dst_ref=landings[stage].at[(slice(None),) * len(free) + (rows,)],
            send_sem=send_sem.at[n, stage],
            recv_sem=recv_sem.at[n, stage],
            device_id=(peers[place],),
            device_id_type=pl.DeviceIdType.MESH,
        )
        copy.start()
        copies[n][stage] = copy

    def add(n, stage):
        order, (low, size) = orders[n], parts[n]
        rows = pl.ds(low, size)
        free = sorted(everything - set(order[: stage + 1]), reverse=True)
        copies[n][stage].wait_recv()

        def one(at, carry):
            values = {}
            for spot, place in enumerate(free):
                values[place] = lax.rem(at // (1 << (len(free) - 1 - spot)), 2)
            full = tuple(
                values[place] if place in values else bit_of(me, place)
                for place in range(places - 1, -1, -1)
            )
            kept = full[:-1] + (rows,)
            landed = landings[stage][tuple(values[place] for place in free) + (rows,)]
            if stage == 0:
                acc[kept] = g_ref[full + (rows,)] + landed
            elif stage < places - 1:
                acc[kept] = acc[kept] + landed
            else:
                out_ref[rows] = acc[kept].astype(f32) + landed.astype(f32)
            return carry

        lax.fori_loop(0, 1 << len(free), one, 0)

    for n in range(len(orders)):
        send(n, 0)
    for stage in range(places):
        for n in range(len(orders)):
            add(n, stage)
            if stage < places - 1:
                send(n, stage + 1)
    for group in copies:
        for copy in group:
            copy.wait_send()


def gather_all(shard, devices):
    places = devices.bit_length() - 1
    count = len(routes(places))
    out = pl.pallas_call(
        functools.partial(gather_kernel, places),
        out_shape=shaped((2,) * places + shard.shape, shard.dtype),
        in_specs=[pl.BlockSpec(memory_space=pltpu.VMEM)],
        out_specs=pl.BlockSpec(memory_space=pltpu.VMEM),
        scratch_shapes=[
            pltpu.SemaphoreType.DMA((count, places)),
            pltpu.SemaphoreType.DMA((count, places)),
            pltpu.SemaphoreType.DMA,
        ],
        compiler_params=pltpu.CompilerParams(
            collective_id=0, has_side_effects=True, vmem_limit_bytes=60 * 1024 * 1024
        ),
    )(shard)
    return out.reshape((devices,) + shard.shape)


def scatter_all(grads, devices):
    places = devices.bit_length() - 1
    count = len(routes(places))
    tail = grads.shape[1:]
    return pl.pallas_call(
        functools.partial(scatter_kernel, places),
        out_shape=shaped(tail, f32),
        in_specs=[pl.BlockSpec(memory_space=pltpu.VMEM)],
        out_specs=pl.BlockSpec(memory_space=pltpu.VMEM),
        scratch_shapes=[pltpu.VMEM((2,) * (places - 1) + tail, bf16)]
        + [pltpu.VMEM((2,) * (places - 1 - stage) + tail, bf16) for stage in range(places)]
        + [
            pltpu.SemaphoreType.DMA((count, places)),
            pltpu.SemaphoreType.DMA((count, places)),
        ],
        compiler_params=pltpu.CompilerParams(
            collective_id=1, has_side_effects=True, vmem_limit_bytes=60 * 1024 * 1024
        ),
    )(grads.reshape((2,) * places + tail))


def run(kernel, outs, args, scratch=(), flops=0):
    size = sum(a.size * a.dtype.itemsize for a in args)
    size += sum(a.size * a.dtype.itemsize for a in outs)
    return pl.pallas_call(
        kernel,
        out_shape=tuple(outs),
        in_specs=[pl.BlockSpec(memory_space=pltpu.VMEM)] * len(args),
        out_specs=tuple([pl.BlockSpec(memory_space=pltpu.VMEM)] * len(outs)),
        scratch_shapes=list(scratch),
        compiler_params=pltpu.CompilerParams(vmem_limit_bytes=60 * 1024 * 1024),
        cost_estimate=pl.CostEstimate(flops=flops, bytes_accessed=size, transcendentals=0),
    )(*args)


def shaped(shape, dtype):
    return jax.ShapeDtypeStruct(tuple(shape), dtype)


def offset_onehot(table_rows):
    places = jnp.arange(WIN * WIN, dtype=jnp.int32)
    row_at = places // WIN
    col_at = places % WIN
    index = (row_at[:, None] - row_at[None, :] + WIN - 1) * (2 * WIN - 1) + (
        col_at[:, None] - col_at[None, :] + WIN - 1
    )
    targets = jnp.arange(table_rows, dtype=jnp.int32)
    return (index.reshape(-1)[:, None] == targets[None, :]).astype(f32)


def token_places(shift_by):
    token = jnp.arange(SIDE * SIDE, dtype=jnp.int32)
    row = (token // SIDE - shift_by) % SIDE
    col = (token % SIDE - shift_by) % SIDE
    window = (row // WIN) * (SIDE // WIN) + col // WIN
    inside = (row % WIN) * WIN + col % WIN
    if shift_by:
        edges = SIDE - WIN, SIDE - shift_by
        a_row = (row >= edges[0]).astype(jnp.int32) + (row >= edges[1]).astype(jnp.int32)
        a_col = (col >= edges[0]).astype(jnp.int32) + (col >= edges[1]).astype(jnp.int32)
        label = 3 * a_row + a_col
    else:
        label = jnp.zeros_like(token)
    mask = jnp.where(label[:, None] == label[None, :], 0.0, mask_fill)
    mask = jnp.where(window[:, None] == window[None, :], mask, outside_fill).astype(f32)
    spread = (inside[:, None] == jnp.arange(WIN * WIN)[None, :]).astype(bf16)
    return mask, spread, spread.T


def local(
    images,
    cotangent,
    counts,
    *shards,
):
    devices = lax.axis_size("fsdp")
    gather_dims = (1, 1, 1, 2, 1, 1, 1, 1, 1, 1, 1, 1, 1)
    large_at = (2, 5, 9, 11)
    small_at = (0, 1, 3, 4, 6, 7, 8, 10, 12)
    flats = [tensor.reshape(-1) for tensor in shards]
    tokens, features = images.shape[1:]
    packed = jnp.concatenate([flats[n] for n in small_at])
    small_rows = 16 * -(-packed.shape[0] // (16 * features))
    packed = jnp.pad(packed, (0, small_rows * features - packed.shape[0]))
    blocks, spans = [packed.reshape(small_rows, features)], {}
    filled = small_rows
    for layer in range(LAYERS):
        for n in large_at:
            piece = shards[n][layer]
            rows, wide = piece.shape[0], piece.shape[1] // features
            piece = piece.reshape(rows, wide, features).transpose(1, 0, 2)
            blocks.append(piece.reshape(rows * wide, features))
            spans[n, layer] = (filled, rows, wide)
            filled += rows * wide
    spare = -filled % 16
    if spare:
        blocks.append(jnp.zeros((spare, features), bf16))
    gathered = gather_all(jnp.concatenate(blocks), devices)
    packed = gathered[:, :small_rows].reshape(devices, -1)
    weights = [None] * len(shards)
    at = 0
    for n in small_at:
        shape, axis_dim = shards[n].shape, gather_dims[n]
        size = flats[n].shape[0]
        piece = packed[:, at : at + size].reshape((devices,) + shape)
        piece = jnp.moveaxis(piece, 0, axis_dim)
        full = shape[:axis_dim] + (devices * shape[axis_dim],) + shape[axis_dim + 1 :]
        weights[n] = piece.reshape(full)
        at += size
    for n in large_at:
        weights[n] = [None] * LAYERS
        for layer in range(LAYERS):
            low, rows, wide = spans[n, layer]
            piece = gathered[:, low : low + rows * wide]
            piece = piece.reshape(devices, wide, rows, features).transpose(1, 0, 2, 3)
            piece = piece.reshape(wide, devices * rows, features)
            weights[n][layer] = piece if wide > 1 else piece[0]
    table = weights[4]
    heads = table.shape[-1]
    hidden = weights[10].shape[-1]
    cells = WIN * WIN
    onehot = offset_onehot(table.shape[1])
    pairs = jnp.einsum("pt,lth->lhp", onehot.astype(bf16), table, preferred_element_type=f32)
    pairs = pairs.reshape(LAYERS, heads, cells, cells).transpose(0, 1, 3, 2).astype(bf16)
    zero = jnp.zeros((features,), f32)

    def row(n, layer):
        return weights[n][layer].astype(f32).reshape(1, -1)

    active = counts[0] > 0
    current = images[0].astype(f32)
    saved = []
    for layer in range(LAYERS):
        mask, spread, spread_t = token_places(SHIFT if layer % 2 else 0)
        bias = run(
            bias_kernel,
            [shaped((heads, tokens, tokens), f32)],
            (pairs[layer], spread, spread_t, mask),
        )[0]
        b_qv = weights[3][layer].astype(f32)
        b_qkv = jnp.concatenate([b_qv[0], zero, b_qv[1]]).reshape(1, -1)
        attn = run(
            attn_fwd_kernel,
            [
                shaped((tokens, features), f32),
                shaped((tokens, features), bf16),
                shaped((tokens, 3 * features), bf16),
                shaped((features, tokens), bf16),
                shaped((heads, tokens, tokens), f32),
                shaped((features, tokens), bf16),
            ],
            (current, row(0, layer), row(1, layer), weights[2][layer], b_qkv, bias,
             weights[5][layer], row(6, layer)),
            [pltpu.VMEM((features, tokens), bf16)],
        )
        mlp = run(
            mlp_fwd_kernel,
            [
                shaped((tokens, features), f32),
                shaped((tokens, features), bf16),
                shaped((tokens, hidden), f32),
                shaped((tokens, hidden), bf16),
            ],
            (attn[0], row(7, layer), row(8, layer), weights[9][layer], row(10, layer),
             weights[11][layer], row(12, layer)),
        )
        saved.append((current, attn, mlp, spread, spread_t))
        current = mlp[0]
    outs = jnp.where(active, current, 0.0)[None]
    grad = jnp.where(active, cotangent[0].astype(f32), 0.0)
    sums = [[None] * LAYERS for _ in shards]
    owned = [[None] * LAYERS for _ in shards]

    def scatter(value):
        return value

    for layer in reversed(range(LAYERS)):
        entry, attn, mlp, spread, spread_t = saved[layer]
        g_mid, g_w1, g_w2, *rest = run(
            mlp_bwd_kernel,
            [
                shaped((tokens, features), f32),
                shaped((hidden // features, features, features), bf16),
                shaped((hidden, features), bf16),
                shaped((1, hidden), f32),
                shaped((1, features), f32),
                shaped((1, features), f32),
                shaped((1, features), f32),
                shaped((1, features), f32),
            ],
            (grad, attn[0], row(7, layer), weights[9][layer], weights[11][layer], *mlp[1:]),
        )
        sums[10][layer], sums[12][layer], sums[7][layer], sums[8][layer], sums[6][layer] = rest
        owned[11][layer] = scatter(g_w2)
        owned[9][layer] = scatter(g_w1)
        grad, g_qkv, g_proj, g_qv, g_pairs, g_gain, g_off = run(
            attn_bwd_kernel,
            [
                shaped((tokens, features), f32),
                shaped((3, features, features), bf16),
                shaped((features, features), bf16),
                shaped((2, features), f32),
                shaped((heads, cells, cells), f32),
                shaped((1, features), f32),
                shaped((1, features), f32),
            ],
            (g_mid, entry, row(0, layer), weights[2][layer], weights[5][layer], *attn[1:],
             spread, spread_t),
            [
                pltpu.VMEM((tokens, features), bf16),
                pltpu.VMEM((features, tokens), f32),
                pltpu.VMEM((tokens, 3 * features), bf16),
            ],
        )
        owned[5][layer] = scatter(g_proj)
        owned[2][layer] = scatter(g_qkv)
        sums[0][layer], sums[1][layer], sums[3][layer] = g_gain, g_off, g_qv
        per_pair = g_pairs.transpose(0, 2, 1).reshape(heads, cells * cells)
        sums[4][layer] = jnp.dot(per_pair, onehot, precision=lax.Precision.HIGHEST).T
    parts = []
    for n in small_at:
        shape, axis_dim = shards[n].shape, gather_dims[n]
        both = jnp.stack(sums[n])
        both = both.reshape(shape[:axis_dim] + (devices,) + shape[axis_dim:])
        parts.append(jnp.moveaxis(both, axis_dim, 0).reshape(devices, -1))
    packed = jnp.concatenate(parts, axis=1).astype(bf16)
    packed = jnp.pad(packed, ((0, 0), (0, small_rows * features - packed.shape[1])))
    blocks = [packed.reshape(devices, small_rows, features)]
    for layer in range(LAYERS):
        for n in large_at:
            low, rows, wide = spans[n, layer]
            piece = owned[n][layer].reshape(wide, devices, rows, features)
            blocks.append(piece.transpose(1, 0, 2, 3).reshape(devices, rows * wide, features))
    if spare:
        blocks.append(jnp.zeros((devices, spare, features), bf16))
    reduced = scatter_all(jnp.concatenate(blocks, axis=1), devices)
    summed = reduced[:small_rows].reshape(-1)
    at = 0
    for n in small_at:
        size = flats[n].shape[0]
        owned[n] = summed[at : at + size].reshape(shards[n].shape)
        at += size
    for n in large_at:
        for layer in range(LAYERS):
            low, rows, wide = spans[n, layer]
            piece = reduced[low : low + rows * wide].reshape(wide, rows, features)
            owned[n][layer] = piece.transpose(1, 0, 2).reshape(rows, wide * features)
        owned[n] = jnp.stack(owned[n])
    return (outs, grad[None], *owned)


def solution(mesh):
    in_specs = (
        P("fsdp", None, None),
        P("fsdp", None, None),
        P("fsdp"),
        P(None, "fsdp"),
        P(None, "fsdp"),
        P(None, "fsdp", None),
        P(None, None, "fsdp"),
        P(None, "fsdp", None),
        P(None, "fsdp", None),
        P(None, "fsdp"),
        P(None, "fsdp"),
        P(None, "fsdp"),
        P(None, "fsdp", None),
        P(None, "fsdp"),
        P(None, "fsdp", None),
        P(None, "fsdp"),
    )
    out_specs = (
        P("fsdp", None, None),
        P("fsdp", None, None),
        P(None, "fsdp"),
        P(None, "fsdp"),
        P(None, "fsdp", None),
        P(None, None, "fsdp"),
        P(None, "fsdp", None),
        P(None, "fsdp", None),
        P(None, "fsdp"),
        P(None, "fsdp"),
        P(None, "fsdp"),
        P(None, "fsdp", None),
        P(None, "fsdp"),
        P(None, "fsdp", None),
        P(None, "fsdp"),
    )
    return jax.shard_map(local, mesh=mesh, in_specs=in_specs, out_specs=out_specs, check_vma=False)
```
